512 devices in a mesh: tm: 16 (over z), tensor: 32 (over y, x, core).
Axes of the slice: x: 4, y: 4, z: 16, core: 2. Of those that a mesh axis runs over, the one named last changes fastest.
Arguments:
- integrals: bfloat16 [1024, 8, 4096], P('tensor'), may hold values from -0.75 to 0.75
- pair_lists: int32 [16, 8], replicated, may hold values from 0 to 31, as said below
- occ_density: bfloat16 [16, 32, 64, 64], P('tm', 'tensor'), may hold values from -0.75 to 0.75
- virt_density: bfloat16 [16, 32, 64, 64], P('tm', 'tensor'), may hold values from -0.75 to 0.75
- cosine_weights: float32 [16, 16], replicated, may hold values from -1.5 to 1.5
- coulomb_blocks: float32 [16, 64, 64], replicated, may hold values from -0.75 to 0.75
Outputs:
- screened: float32 [16, 1024, 1024], P('tm', 'tensor')
The draws below stay inside these ranges and needn't reach their ends.
Inputs may be any that keep to these rules, and one draw needn't show every extreme that they name: `pair_lists`: row p names the 8 pair blocks listed with aux block p, all different, in ascending order. Every pair block is named in 1 to 6 rows, and some pair block in exactly 6 rows.
All inputs are finite; a program needn't handle non-finite values.
Results may differ from the reference program's by a relative error of at most 0.01.
Values may be sent and summed in bfloat16 or wider, within the bound.
A program may use at most 64 MiB of HBM per device.

```python
import jax
import jax.numpy as jnp
from jax import lax

SLAB = 1024
AUXB = 64
ORB = 64
MOST = 6
TIMES = 16
FREQS = 16
PB = 16
PAIRS = 32
CAPS = 8


def draw_pair_lists(key, part):
    key_order = jax.random.fold_in(key, 11)
    key_caps = jax.random.fold_in(key, 23)
    key_label = jax.random.fold_in(key, 37)
    order = jax.random.permutation(key_order, PAIRS).astype(jnp.int32)
    removable = jax.random.randint(key_caps, (PAIRS,), 3, MOST, dtype=jnp.int32)
    removable = removable.at[0].set(0)
    excess = PAIRS * MOST - PB * CAPS
    before = jnp.cumsum(removable) - removable
    removed = jnp.clip(excess - before, 0, removable)
    counts = jnp.zeros((PAIRS,), jnp.int32).at[order].set(MOST - removed)
    ends = jnp.cumsum(counts)
    slot_ids = jnp.arange(PB * CAPS, dtype=jnp.int32)
    owners = jnp.sum((ends[None, :] <= slot_ids[:, None]).astype(jnp.int32), axis=1)
    table = owners.reshape(CAPS, PB).T
    relabel = jax.random.permutation(key_label, PB)
    return table[relabel].astype(jnp.int32)


def block_scale(rng, shape, shards, smallest, high):
    def one(axis_at, parts):
        steps = jax.random.uniform(jax.random.fold_in(jax.random.fold_in(rng, 6), axis_at), (parts,), jnp.float32, smallest / len(shards), high / len(shards))
        return jnp.repeat(jnp.exp(steps), shape[axis_at] // parts).reshape((-1,) + (1,) * (len(shape) - axis_at - 1))

    level = one(*shards[0])
    for cut in shards[1:]:
        level = level * one(*cut)
    return level


def gaussian(stream_key, shape, scale, bound, cuts=(), kind=jnp.bfloat16):
    loudness = block_scale(stream_key, shape, cuts, -0.22, 0.18) if cuts else 1.0
    array = jax.random.normal(stream_key, shape, jnp.float32) * scale * loudness
    return jnp.minimum(jnp.maximum(array, -bound), bound).astype(kind)


def setup_inputs(seed: int = 0) -> dict:
    seeds = jax.random.split(jax.random.key(seed), 7)
    integrals = gaussian(seeds[0], (SLAB, CAPS, ORB * ORB), 0.125, 0.75, ((0, 32),))
    pair_lists = draw_pair_lists(jax.random.fold_in(seeds[6], 71), 0)
    occ_density = gaussian(seeds[2], (TIMES, PAIRS, ORB, ORB), ORB ** -0.5, 0.75, ((0, 16), (1, 32)))
    virt_density = gaussian(seeds[3], (TIMES, PAIRS, ORB, ORB), ORB ** -0.5, 0.75, ((0, 16), (1, 32)))
    cosine_weights = gaussian(seeds[4], (FREQS, TIMES), TIMES ** -0.5, 1.5, (), jnp.float32)
    coulomb_blocks = gaussian(seeds[5], (PB, AUXB, AUXB), AUXB ** -0.5, 0.75, (), jnp.float32)
    return dict(integrals=integrals, pair_lists=pair_lists, occ_density=occ_density, virt_density=virt_density, cosine_weights=cosine_weights, coulomb_blocks=coulomb_blocks)


def listed_blocks(pair_lists, pair_index):
    block_count = pair_lists.shape[0]
    member = jnp.any(pair_lists == pair_index, axis=1)
    positions = jnp.cumsum(member.astype(jnp.int32)) - 1
    slot_ids = jnp.arange(MOST, dtype=jnp.int32)
    matches = member[None, :] & (positions[None, :] == slot_ids[:, None])
    labels = jnp.arange(block_count, dtype=jnp.int32)
    located = jnp.sum(jnp.where(matches, labels[None, :], 0), axis=1).astype(jnp.int32)
    return jnp.where(jnp.any(matches, axis=1), located, block_count).astype(jnp.int32)


def density_product(row_data, occupied, virtual):
    row_count = row_data.shape[0]
    orbital_width = occupied.shape[0]
    half_done = jnp.dot(row_data.reshape(row_count * orbital_width, orbital_width), virtual, preferred_element_type=jnp.float32)
    half_done = half_done.astype(jnp.bfloat16).reshape(row_count, orbital_width, orbital_width)
    contracted = jnp.einsum("rms,ml->rls", half_done.astype(jnp.float32), occupied.astype(jnp.float32))
    return contracted.astype(jnp.bfloat16).reshape(row_count, orbital_width * orbital_width)


def pair_column(integrals, pair_lists, pair_index):
    row_block = jnp.arange(SLAB, dtype=jnp.int32) // AUXB
    chosen = pair_lists[row_block] == pair_index
    list_pos = jnp.sum(jnp.where(chosen, jnp.arange(CAPS, dtype=jnp.int32)[None, :], 0), axis=1).astype(jnp.int32)
    picked = jnp.take_along_axis(integrals, list_pos[:, None, None], axis=1)[:, 0]
    return jnp.where(jnp.any(chosen, axis=1)[:, None], picked, jnp.zeros_like(picked))


def reference(integrals, pair_lists, occ_density, virt_density, cosine_weights, coulomb_blocks):
    pair_ids = jnp.arange(PAIRS, dtype=jnp.int32)

    def one_time(time_step):
        def one_pair(chi_sum, pair_index):
            column = pair_column(integrals, pair_lists, pair_index)
            chosen = listed_blocks(pair_lists, pair_index)
            wanted = (chosen[:, None] * AUXB + jnp.arange(AUXB, dtype=jnp.int32)[None, :]).reshape(-1)
            tile_rows = jnp.take(column, wanted, axis=0, mode="fill", fill_value=0)
            weighted = density_product(tile_rows, occ_density[time_step, pair_index], virt_density[time_step, pair_index])
            gram_block = jnp.dot(weighted, tile_rows.T, preferred_element_type=jnp.float32)
            rounded = lax.optimization_barrier(gram_block.astype(jnp.bfloat16)).astype(jnp.float32)
            squares = rounded.reshape(MOST, AUXB, MOST, AUXB).transpose(0, 2, 1, 3)
            chi_sum = chi_sum.at[chosen[:, None], :, chosen[None, :], :].add(squares, mode="drop")
            return chi_sum, None

        start_sum = jnp.zeros((PB, AUXB, PB, AUXB), jnp.float32)
        chi_sum, unused = lax.scan(one_pair, start_sum, pair_ids)
        return chi_sum.reshape(SLAB, SLAB)

    chi_time = lax.map(one_time, jnp.arange(TIMES, dtype=jnp.int32))
    chi_freq = jnp.einsum("ft,tab->fab", cosine_weights, chi_time, precision=lax.Precision.HIGHEST)
    shaped = chi_freq.reshape(FREQS, SLAB, PB, AUXB)
    screened = jnp.einsum("frpa,pab->frpb", shaped, coulomb_blocks, precision=lax.Precision.HIGHEST)
    return screened.reshape(FREQS, SLAB, SLAB)
```

```python
import jax
import jax.numpy as jnp
from jax import lax
from jax.experimental import pallas as pl
from jax.experimental.pallas import tpu as pltpu
from jax.sharding import PartitionSpec as P

MESH = pl.DeviceIdType.MESH
MOST = 6
PB = 16
ORB = 64
ROWS = 32
PAIRS = 32
TIMES = 16
WIDTH = 256
SLOTS = MOST * 64
NT = (((1,), (1,)), ((), ()))
TN = (((0,), (0,)), ((), ()))


def tables(pair_lists, me, listed):
    ks = jnp.concatenate([me[None], listed])
    member = jnp.any(pair_lists[None] == ks[:, None, None], axis=2)
    before = jnp.arange(PB)[None, :] < jnp.arange(PB)[:, None]
    rank = jnp.sum((member[:, None, :] & before[None]).astype(jnp.int32), axis=2)
    labels = jnp.arange(PB, dtype=jnp.int32)
    hit = member[0][None, :] & (rank[0][None, :] == jnp.arange(MOST)[:, None])
    chosen = PB - jnp.sum(jnp.where(hit, PB - labels[None, :], 0), axis=1)
    slot_of = jnp.where(member[0], rank[0], 0)
    places = jnp.where(member[1:], listed[:, None] * MOST + rank[1:], PAIRS * MOST)
    return chosen.astype(jnp.int32), slot_of.astype(jnp.int32), places.astype(jnp.int32)


def iota(shape, axis):
    return lax.broadcasted_iota(jnp.int32, shape, axis)


def gather_kernel(chosen_ref, stage_ref, t_ref, got, comp, send1, recv1, sendz, recvz):
    z = lax.axis_index("tm")
    me = lax.axis_index("tensor")
    right, left = lax.rem(z + 1, TIMES), lax.rem(z + TIMES - 1, TIMES)

    barrier = pltpu.get_barrier_semaphore()

    def greet(i, carry):
        pl.semaphore_signal(
            barrier, inc=1, device_id={"tensor": lax.rem(me + i, PAIRS)}, device_id_type=MESH
        )
        return carry

    lax.fori_loop(1, PAIRS, greet, 0)
    for side in (left, right):
        pl.semaphore_signal(barrier, inc=1, device_id={"tm": side}, device_id_type=MESH)
    pl.semaphore_wait(barrier, PAIRS + 1)

    block = lax.div(me, 2)
    first = pl.multiple_of(lax.rem(me, 2) * ROWS, ROWS)

    def exchange(i):
        peer = lax.rem(me + i, PAIRS)
        return pltpu.make_async_remote_copy(
            src_ref=stage_ref.at[peer],
            dst_ref=got.at[block, pl.ds(first, ROWS)],
            send_sem=send1.at[i],
            recv_sem=recv1.at[i],
            device_id={"tensor": peer},
            device_id_type=MESH,
        )

    def start(i, carry):
        exchange(i).start()
        return carry

    lax.fori_loop(1, PAIRS, start, 0)
    got[PB] = jnp.zeros((64, WIDTH), jnp.bfloat16)
    got[block, pl.ds(first, ROWS)] = stage_ref[me]
    unit = (iota((WIDTH, WIDTH), 0) == iota((WIDTH, WIDTH), 1)).astype(jnp.float32)
    unit = unit.astype(jnp.bfloat16)

    def finish(i, carry):
        exchange(i).wait()
        return carry

    lax.fori_loop(1, PAIRS, finish, 0)
    for j in range(MOST):
        comp[64 * j : 64 * j + 64] = got[chosen_ref[j]]
    own = lax.dot_general(unit, comp[...], NT, preferred_element_type=jnp.float32)
    t_ref[pl.ds(4 * z, 4)] = own.astype(jnp.bfloat16).reshape(4, ORB, SLOTS)

    def hop(way, step, half):
        owner = lax.rem(z + (TIMES - (step - 1) if way == 0 else step - 1), TIMES)
        piece = t_ref.at[pl.ds(4 * owner + 2 * half, 2)]
        return pltpu.make_async_remote_copy(
            src_ref=piece,
            dst_ref=piece,
            send_sem=sendz.at[way, step - 1, half],
            recv_sem=recvz.at[way, step - 1, half],
            device_id={"tm": right if way == 0 else left},
            device_id_type=MESH,
        )

    last = TIMES // 2
    for step in range(1, last + 1):
        for half in range(2):
            for way in range(2):
                if step > 1:
                    hop(way, step - 1, half).wait_recv()
                if step < last or half == way:
                    hop(way, step, half).start()
    for way in range(2):
        hop(way, last, way).wait_recv()
    for step in range(1, last + 1):
        for half in range(2):
            for way in range(2):
                if step < last or half == way:
                    hop(way, step, half).wait_send()


def term_kernel(
    chosen_ref, slot_ref, t_ref, occ_ref, virt_ref, left_ref, right_ref, out_ref,
    ko, kv, half, gram, lead, trail, folded,
):
    big, small = ORB * 16, ORB * 4
    pick = (lax.div(iota((big, ORB), 0), 16) == iota((big, ORB), 1)).astype(jnp.float32)
    pick = pick.astype(jnp.bfloat16)
    rows = lax.dot_general(pick, occ_ref[...], NT, preferred_element_type=jnp.float32)
    full = lax.dot_general(
        rows.astype(jnp.bfloat16), pick, NT, preferred_element_type=jnp.float32
    )
    same = lax.rem(iota((big, big), 0), 16) == lax.rem(iota((big, big), 1), 16)
    ko[...] = jnp.where(same, full, 0.0).astype(jnp.bfloat16)
    pick = (lax.rem(iota((small, ORB), 0), ORB) == iota((small, ORB), 1)).astype(jnp.float32)
    pick = pick.astype(jnp.bfloat16)
    rows = lax.dot_general(pick, virt_ref[...], NT, preferred_element_type=jnp.float32)
    full = lax.dot_general(
        rows.astype(jnp.bfloat16), pick, NT, preferred_element_type=jnp.float32
    )
    same = lax.div(iota((small, small), 0), ORB) == lax.div(iota((small, small), 1), ORB)
    kv[...] = jnp.where(same, full, 0.0).astype(jnp.bfloat16)

    lead[...] = jnp.zeros_like(lead)
    trail[...] = jnp.zeros_like(trail)
    for j in range(MOST):
        block = jnp.minimum(chosen_ref[j], PB - 1)
        lead[64 * j : 64 * j + 64, 128 * j : 128 * j + 128] = left_ref[block]
        trail[64 * j : 64 * j + 64, 128 * j : 128 * j + 128] = right_ref[block]

    def occupied(g, carry):
        nus = pl.ds(pl.multiple_of(g * 16, 16), 16)
        part = jnp.dot(
            ko[...], t_ref[:, nus, :].reshape(big, SLOTS), preferred_element_type=jnp.float32
        )
        half[:, nus, :] = part.astype(jnp.bfloat16).reshape(ORB, 16, SLOTS)
        return carry

    lax.fori_loop(0, 4, occupied, 0)
    gram[...] = jnp.zeros_like(gram)

    def virtual(b, carry):
        lams = pl.ds(b * 4, 4)
        mixed = jnp.dot(
            kv[...], half[lams].reshape(small, SLOTS), preferred_element_type=jnp.float32
        )
        gram[...] += lax.dot_general(
            mixed.astype(jnp.bfloat16), t_ref[lams].reshape(small, SLOTS), TN,
            preferred_element_type=jnp.float32,
        )
        return carry

    lax.fori_loop(0, 16, virtual, 0)
    term = gram[...].astype(jnp.bfloat16)
    upper = jnp.dot(term, lead[...], preferred_element_type=jnp.float32)
    lower = jnp.dot(term, trail[...], preferred_element_type=jnp.float32)
    for b in range(2 * MOST):
        both = upper[32 * b : 32 * b + 16] + lower[32 * b + 16 : 32 * b + 32]
        both = both.astype(jnp.bfloat16)
        for j in range(MOST):
            folded[b, j] = both[:, 128 * j : 128 * j + 128]
    for d in range(PAIRS):
        out_ref[d] = folded[slot_ref[d // 2] * 2 + d % 2]


def merge_kernel(
    place_ref, cos_ref, term_ref, out_ref, got, chi, times, spread, freqs,
    send1, recv1, send2, recv2, send3, recv3,
):
    z = lax.axis_index("tm")
    me = lax.axis_index("tensor")
    barrier = pltpu.get_barrier_semaphore()

    def greet(i, carry):
        pl.semaphore_signal(
            barrier, inc=1, device_id={"tensor": lax.rem(me + i, PAIRS)}, device_id_type=MESH
        )
        return carry

    def greet_far(i, carry):
        pl.semaphore_signal(
            barrier, inc=1, device_id={"tm": lax.rem(z + i, TIMES)}, device_id_type=MESH
        )
        return carry

    lax.fori_loop(1, TIMES, greet_far, 0)
    lax.fori_loop(1, PAIRS, greet, 0)
    pl.semaphore_wait(barrier, PAIRS + TIMES - 2)

    def exchange(i):
        peer = lax.rem(me + i, PAIRS)
        return pltpu.make_async_remote_copy(
            src_ref=term_ref.at[peer],
            dst_ref=got.at[pl.ds(me * MOST, MOST)],
            send_sem=send1.at[i],
            recv_sem=recv1.at[i],
            device_id={"tensor": peer},
            device_id_type=MESH,
        )

    def start(i, carry):
        exchange(i).start()
        return carry

    def finish(i, carry):
        exchange(i).wait()
        return carry

    lax.fori_loop(1, PAIRS, start, 0)
    got[PAIRS * MOST] = jnp.zeros((16, 128), jnp.bfloat16)
    got[pl.ds(me * MOST, MOST)] = term_ref[me]
    lax.fori_loop(1, PAIRS, finish, 0)

    for q in range(PB):
        total = got[place_ref[0, q]].astype(jnp.float32)
        for c in range(1, 8):
            total += got[place_ref[c, q]].astype(jnp.float32)
        chi[q] = total.astype(jnp.bfloat16)

    def trade(src, dst, send, recv):
        def one(i):
            peer = lax.rem(z + i, TIMES)
            return pltpu.make_async_remote_copy(
                src_ref=src.at[peer],
                dst_ref=dst.at[z],
                send_sem=send.at[i],
                recv_sem=recv.at[i],
                device_id={"tm": peer},
                device_id_type=MESH,
            )

        def begin(i, carry):
            one(i).start()
            return carry

        def end(i, carry):
            one(i).wait()
            return carry

        lax.fori_loop(1, TIMES, begin, 0)
        dst[z] = src[z]
        lax.fori_loop(1, TIMES, end, 0)

    trade(chi, times, send2, recv2)
    series = [times[t].astype(jnp.float32) for t in range(TIMES)]
    for f in range(TIMES):
        total = cos_ref[f, 0] * series[0]
        for t in range(1, TIMES):
            total += cos_ref[f, t] * series[t]
        spread[f] = total.astype(jnp.bfloat16)
    trade(spread, freqs, send3, recv3)

    low = iota((16, 128), 1) < 64
    for m in range(PB // 2):
        even = freqs[2 * m].astype(jnp.float32)
        odd = freqs[2 * m + 1].astype(jnp.float32)
        lanes = slice(128 * m, 128 * m + 128)
        out_ref[0, 0:16, lanes] = jnp.where(low, even, pltpu.roll(odd, 64, 1))
        out_ref[0, 16:32, lanes] = jnp.where(low, pltpu.roll(even, 64, 1), odd)


def per_device(integrals, pair_lists, occ_density, virt_density, cosine_weights, coulomb_blocks):
    z = lax.axis_index("tm")
    me = lax.axis_index("tensor")
    listed = lax.dynamic_index_in_dim(pair_lists, me // 2, 0, keepdims=False)
    chosen, slot_of, places = tables(pair_lists, me, listed)

    mine = lax.dynamic_slice_in_dim(integrals, z * WIDTH, WIDTH, axis=2).reshape(ROWS * 8, WIDTH)
    wide = (PAIRS, ROWS, ROWS, 8)
    route = (iota(wide, 1) == iota(wide, 2)) & (iota(wide, 0) == listed[None, None, None, :])
    stage = jnp.dot(
        route.reshape(PAIRS * ROWS, ROWS * 8).astype(jnp.bfloat16),
        mine,
        preferred_element_type=jnp.float32,
    )
    stage = stage.astype(jnp.bfloat16).reshape(PAIRS, ROWS, WIDTH)
    factor = coulomb_blocks.astype(jnp.bfloat16)
    left_factor = jnp.pad(factor, ((0, 0), (0, 0), (0, 64)))
    right_factor = jnp.pad(factor, ((0, 0), (0, 0), (64, 0)))

    smem = pl.BlockSpec(memory_space=pltpu.SMEM)
    vmem = pl.BlockSpec(memory_space=pltpu.VMEM)
    dma = pltpu.SemaphoreType.DMA
    tiles = pl.pallas_call(
        gather_kernel,
        out_shape=jax.ShapeDtypeStruct((ORB, ORB, SLOTS), jnp.bfloat16),
        in_specs=[smem, vmem],
        out_specs=vmem,
        scratch_shapes=[
            pltpu.VMEM((PB + 1, 64, WIDTH), jnp.bfloat16),
            pltpu.VMEM((SLOTS, WIDTH), jnp.bfloat16),
            dma((PAIRS,)),
            dma((PAIRS,)),
            dma((2, 8, 2)),
            dma((2, 8, 2)),
        ],
        compiler_params=pltpu.CompilerParams(collective_id=0, has_side_effects=True),
        name="gather_tiles",
    )(chosen, stage)
    terms = pl.pallas_call(
        term_kernel,
        out_shape=jax.ShapeDtypeStruct((PAIRS, MOST, 16, 128), jnp.bfloat16),
        in_specs=[smem, smem, vmem, vmem, vmem, vmem, vmem],
        out_specs=vmem,
        scratch_shapes=[
            pltpu.VMEM((1024, 1024), jnp.bfloat16),
            pltpu.VMEM((256, 256), jnp.bfloat16),
            pltpu.VMEM((ORB, ORB, SLOTS), jnp.bfloat16),
            pltpu.VMEM((SLOTS, SLOTS), jnp.float32),
            pltpu.VMEM((SLOTS, 2 * SLOTS), jnp.bfloat16),
            pltpu.VMEM((SLOTS, 2 * SLOTS), jnp.bfloat16),
            pltpu.VMEM((2 * MOST, MOST, 16, 128), jnp.bfloat16),
        ],
        name="pair_terms",
    )(
        chosen, slot_of, tiles, occ_density[0, 0], virt_density[0, 0], left_factor, right_factor
    )
    block = pltpu.VMEM((PB, 16, 128), jnp.bfloat16)
    return pl.pallas_call(
        merge_kernel,
        out_shape=jax.ShapeDtypeStruct((1, ROWS, PB * 64), jnp.float32),
        in_specs=[smem, smem, vmem],
        out_specs=vmem,
        scratch_shapes=[
            pltpu.VMEM((PAIRS * MOST + 1, 16, 128), jnp.bfloat16),
            block,
            block,
            block,
            block,
            dma((PAIRS,)),
            dma((PAIRS,)),
            dma((TIMES,)),
            dma((TIMES,)),
            dma((TIMES,)),
            dma((TIMES,)),
        ],
        compiler_params=pltpu.CompilerParams(collective_id=1, has_side_effects=True),
        name="merge_terms",
    )(places, cosine_weights, terms)


def solution(mesh):
    in_specs = (
        P("tensor", None, None),
        P(),
        P("tm", "tensor", None, None),
        P("tm", "tensor", None, None),
        P(),
        P(),
    )
    return jax.shard_map(
        per_device, mesh=mesh, in_specs=in_specs, out_specs=P("tm", "tensor", None), check_vma=False
    )
```

```python
import jax
import jax.numpy as jnp
from jax import lax
from jax.experimental import pallas as pl
from jax.experimental.pallas import tpu as pltpu
from jax.sharding import PartitionSpec as P

MESH = pl.DeviceIdType.MESH
MOST = 6
PB = 16
CAPS = 8
ORB = 64
ROWS = 32
PAIRS = 32
TIMES = 16
WIDTH = 256
SLOTS = MOST * 64
STEPS = 6
CHUNKS = 2
NT = (((1,), (1,)), ((), ()))
TN = (((0,), (0,)), ((), ()))
ORDER = (0, 1, -1, 2, -2, 3, -3, 8, 4, -4, 7, 5, -5, -7, 6, -6)
PLACE = {distance: place for place, distance in enumerate(ORDER)}
DIRECT = (0, 8, 7, -7)


def iota(shape, axis):
    return lax.broadcasted_iota(jnp.int32, shape, axis)


def one_hot(mask):
    return mask.astype(jnp.float32).astype(jnp.bfloat16)


def mul(a, b, dims=None):
    if dims is None:
        return jnp.dot(a, b, preferred_element_type=jnp.float32)
    return lax.dot_general(a, b, dims, preferred_element_type=jnp.float32)


def low(x):
    return x.astype(jnp.bfloat16)


def kernel(
    lists_ref, cos_ref, rows_ref, factor_ref, occ_ref, virt_ref, out_ref,
    mine, route, stage, got0, got1, got2, got3, comp, tiles, factor, ko, kv, lead, trail, part, half, gram, folded,
    terms, inbox, chi, times, spread, freqs, places,
    load_sem, factor_sem, send1, recv1, sendz, recvz, send2, recv2, send3, recv3, send4, recv4,
):
    z = lax.axis_index("tm")
    me = lax.axis_index("tensor")
    got = (got0, got1, got2, got3)
    block = lax.div(me, 2)
    first = pl.multiple_of(lax.rem(me, 2) * ROWS, ROWS)

    def at(distance):
        return lax.rem(z + distance + TIMES, TIMES)

    def load(e):
        columns = pl.ds(pl.multiple_of(at(DIRECT[e]) * WIDTH, WIDTH), WIDTH)
        return pltpu.make_async_copy(rows_ref.at[:, columns], mine.at[e], load_sem.at[e])

    for e in range(len(DIRECT)):
        load(e).start()
    fetch = pltpu.make_async_copy(factor_ref, factor, factor_sem)
    fetch.start()

    barrier = pltpu.get_barrier_semaphore()

    def greet(i, carry):
        peer = lax.rem(me + i, PAIRS)
        pl.semaphore_signal(barrier, inc=1, device_id={"tensor": peer}, device_id_type=MESH)
        return carry

    for distance in (2, -2, 1, -1):
        pl.semaphore_signal(barrier, inc=1, device_id={"tm": at(distance)}, device_id_type=MESH)
    lax.fori_loop(1, PAIRS, greet, 0)

    column = lax.rem(iota((1, WIDTH), 1), CAPS)
    names = jnp.full((1, WIDTH), -1, jnp.int32)
    for c in range(CAPS):
        names = jnp.where(column == c, lists_ref[c, block], names)
    shape = (PAIRS * ROWS, WIDTH)
    listed = lax.div(iota(shape, 0), ROWS) == names
    same = lax.rem(iota(shape, 0), ROWS) == lax.div(iota(shape, 1), CAPS)
    route[...] = one_hot(listed & same)

    def pack(e):
        load(e).wait()
        stage[e] = low(mul(route[...], mine[e])).reshape(PAIRS, ROWS, WIDTH)

    pack(0)
    pl.semaphore_wait(barrier, PAIRS + 3)

    def exchange(e, i):
        peer = lax.rem(me + i, PAIRS)
        return pltpu.make_async_remote_copy(
            src_ref=stage.at[e, peer],
            dst_ref=got[e].at[block, pl.ds(first, ROWS)],
            send_sem=send1.at[e, i],
            recv_sem=recv1.at[e, i],
            device_id={"tensor": peer},
            device_id_type=MESH,
        )

    def send_rows(e):
        def start(i, carry):
            exchange(e, i).start()
            return carry

        lax.fori_loop(1, PAIRS, start, 0)

    send_rows(0)

    members, ranks, count = [], [], jnp.int32(0)
    for p in range(PB):
        named = lists_ref[0, p] == me
        for c in range(1, CAPS):
            named = named | (lists_ref[c, p] == me)
        members.append(named)
        ranks.append(count)
        count = count + named.astype(jnp.int32)
    chosen = []
    for j in range(MOST):
        found = jnp.int32(PB)
        for p in range(PB):
            found = jnp.where(members[p] & (ranks[p] == j), p, found)
        chosen.append(found)
    slot_of = [jnp.where(members[p], jnp.minimum(ranks[p], MOST - 1), 0) for p in range(PB)]

    for e in range(len(DIRECT)):
        got[e][PB] = jnp.zeros((64, WIDTH), jnp.bfloat16)
        if e:
            pack(e)
        got[e][block, pl.ds(first, ROWS)] = stage[e, me]
    unit = one_hot(iota((WIDTH, WIDTH), 0) == iota((WIDTH, WIDTH), 1))

    square = (ORB, ORB)
    held = lax.div(iota(square, 0), 4)
    owner = jnp.zeros(square, jnp.int32)
    for place, distance in enumerate(ORDER):
        owner = jnp.where(held == place, at(distance), owner)
    order = one_hot(iota(square, 1) == 4 * owner + lax.rem(iota(square, 0), 4))
    occ = low(mul(low(mul(order, occ_ref[...])), order, NT))
    big, small = ORB * 16, ORB * 4
    pick = one_hot(lax.div(iota((big, ORB), 0), 16) == iota((big, ORB), 1))
    full = mul(low(mul(pick, occ, NT)), pick, NT)
    same = lax.rem(iota((big, big), 0), 16) == lax.rem(iota((big, big), 1), 16)
    ko[...] = low(jnp.where(same, full, 0.0))
    pick = one_hot(lax.rem(iota((small, ORB), 0), ORB) == iota((small, ORB), 1))
    full = mul(low(mul(pick, virt_ref[...], NT)), pick, NT)
    same = lax.div(iota((small, small), 0), ORB) == lax.div(iota((small, small), 1), ORB)
    kv[...] = low(jnp.where(same, full, 0.0))

    def take_rows(e):
        def finish(i, carry):
            exchange(e, i).wait()
            return carry

        lax.fori_loop(1, PAIRS, finish, 0)
        for j in range(MOST):
            comp[64 * j : 64 * j + 64] = got[e][chosen[j]]
        place = PLACE[DIRECT[e]]
        tiles[4 * place : 4 * place + 4] = low(mul(unit, comp[...], NT)).reshape(4, ORB, SLOTS)

    def hop(way, step, chunk):
        sign = -1 if way == 0 else 1
        rows = 4 // CHUNKS
        source = 4 * PLACE[sign * (step - 1)] + rows * chunk
        target = 4 * PLACE[sign * step] + rows * chunk
        return pltpu.make_async_remote_copy(
            src_ref=tiles.at[source : source + rows],
            dst_ref=tiles.at[target : target + rows],
            send_sem=sendz.at[way, step - 1, chunk],
            recv_sem=recvz.at[way, step - 1, chunk],
            device_id={"tm": at(-sign)},
            device_id_type=MESH,
        )

    def contract(b, g0, g1):
        def one(g, carry):
            nus = pl.ds(pl.multiple_of(g * 16, 16), 16)
            x = tiles[16 * b : 16 * b + 16, nus, :].reshape(WIDTH, SLOTS)
            y = mul(ko[:, WIDTH * b : WIDTH * b + WIDTH], x)
            if b == 0:
                part[g] = y
            elif b < 3:
                part[g] += y
            else:
                half[:, nus, :] = low(part[g] + y).reshape(ORB, 16, SLOTS)
            return carry

        lax.fori_loop(g0, g1, one, 0)

    def factors():
        fetch.wait()
        lead[...] = jnp.zeros_like(lead)
        trail[...] = jnp.zeros_like(trail)
        wide = (ORB, 2 * ORB)
        ahead = one_hot(iota(wide, 0) == iota(wide, 1))
        behind = one_hot(iota(wide, 0) + ORB == iota(wide, 1))
        for j in range(MOST):
            value = low(factor[jnp.minimum(chosen[j], PB - 1)])
            lead[64 * j : 64 * j + 64, 128 * j : 128 * j + 128] = low(mul(value, ahead))
            trail[64 * j : 64 * j + 64, 128 * j : 128 * j + 128] = low(mul(value, behind))

    take_rows(0)
    under = {
        (1, 1): factors,
        (3, 1): lambda: contract(0, 0, 2),
        (4, 0): lambda: contract(0, 2, 4),
        (4, 1): lambda: take_rows(1),
        (5, 0): lambda: contract(1, 0, 2),
        (5, 1): lambda: contract(1, 2, 4),
        (6, 0): lambda: take_rows(2),
        (6, 1): lambda: contract(2, 0, 4),
    }
    for step in range(1, STEPS + 1):
        for chunk in range(CHUNKS):
            for way in range(2):
                if step > 1:
                    hop(way, step - 1, chunk).wait_recv()
                hop(way, step, chunk).start()
            if step == 1 and chunk == CHUNKS - 1:
                for e in range(1, len(DIRECT)):
                    send_rows(e)
            if (step, chunk) in under:
                under[step, chunk]()
    take_rows(3)
    for chunk in range(CHUNKS):
        for way in range(2):
            hop(way, STEPS, chunk).wait_recv()
    contract(3, 0, 4)
    gram[...] = jnp.zeros_like(gram)

    def virtual(b, carry):
        lams = pl.ds(b * 4, 4)
        mixed = low(mul(kv[...], half[lams].reshape(small, SLOTS)))
        gram[...] += mul(mixed, tiles[lams].reshape(small, SLOTS), TN)
        return carry

    lax.fori_loop(0, ORB // 4, virtual, 0)
    term = low(gram[...])
    upper, lower = mul(term, lead[...]), mul(term, trail[...])
    for b in range(2 * MOST):
        both = low(upper[32 * b : 32 * b + 16] + lower[32 * b + 16 : 32 * b + 32])
        for j in range(MOST):
            folded[b, j] = both[:, 128 * j : 128 * j + 128]
    for d in range(PAIRS):
        terms[d] = folded[slot_of[d // 2] * 2 + d % 2]

    def trade(axis, count, src, dst, send, recv):
        here = lax.axis_index(axis)

        def one(i):
            peer = lax.rem(here + i, count)
            return pltpu.make_async_remote_copy(
                src_ref=src.at[peer],
                dst_ref=dst.at[here],
                send_sem=send.at[i],
                recv_sem=recv.at[i],
                device_id={axis: peer},
                device_id_type=MESH,
            )

        def begin(i, carry):
            one(i).start()
            return carry

        def end(i, carry):
            one(i).wait()
            return carry

        lax.fori_loop(1, count, begin, 0)
        dst[here] = src[here]
        return lambda: lax.fori_loop(1, count, end, 0)

    arrive = trade("tensor", PAIRS, terms, inbox, send2, recv2)
    inbox[PAIRS, 0] = jnp.zeros((16, 128), jnp.bfloat16)

    def locate(c, carry):
        name = lists_ref[c, block]
        rank = jnp.int32(0)
        for q in range(PB):
            named = lists_ref[0, q] == name
            for other in range(1, CAPS):
                named = named | (lists_ref[other, q] == name)
            places[0, c * PB + q] = jnp.where(named, name, PAIRS)
            places[1, c * PB + q] = jnp.where(named, jnp.minimum(rank, MOST - 1), 0)
            rank = rank + named.astype(jnp.int32)
        return carry

    lax.fori_loop(0, CAPS, locate, 0)
    for step in range(1, STEPS + 1):
        for chunk in range(CHUNKS):
            for way in range(2):
                hop(way, step, chunk).wait_send()
    arrive()
    for q in range(PB):
        total = inbox[places[0, q], places[1, q]].astype(jnp.float32)
        for c in range(1, CAPS):
            spot = c * PB + q
            total += inbox[places[0, spot], places[1, spot]].astype(jnp.float32)
        chi[q] = low(total)

    trade("tm", TIMES, chi, times, send3, recv3)()
    series = [times[t].astype(jnp.float32) for t in range(TIMES)]
    for f in range(TIMES):
        total = cos_ref[f, 0] * series[0]
        for t in range(1, TIMES):
            total += cos_ref[f, t] * series[t]
        spread[f] = low(total)
    trade("tm", TIMES, spread, freqs, send4, recv4)()

    near = iota((16, 128), 1) < 64
    for m in range(PB // 2):
        even = freqs[2 * m].astype(jnp.float32)
        odd = freqs[2 * m + 1].astype(jnp.float32)
        lanes = slice(128 * m, 128 * m + 128)
        out_ref[0, 0:16, lanes] = jnp.where(near, even, pltpu.roll(odd, 64, 1))
        out_ref[0, 16:32, lanes] = jnp.where(near, pltpu.roll(even, 64, 1), odd)


def per_device(integrals, pair_lists, occ_density, virt_density, cosine_weights, coulomb_blocks):
    smem = pl.BlockSpec(memory_space=pltpu.SMEM)
    vmem = pl.BlockSpec(memory_space=pltpu.VMEM)
    hbm = pl.BlockSpec(memory_space=pl.ANY)
    dma = pltpu.SemaphoreType.DMA
    half = jnp.bfloat16
    direct = len(DIRECT)
    block = pltpu.VMEM((PB, 16, 128), half)
    arrived = pltpu.VMEM((PB + 1, 64, WIDTH), half)
    return pl.pallas_call(
        kernel,
        out_shape=jax.ShapeDtypeStruct((1, ROWS, PB * 64), jnp.float32),
        in_specs=[smem, smem, hbm, hbm, vmem, vmem],
        out_specs=vmem,
        scratch_shapes=[
            pltpu.VMEM((direct, ROWS * CAPS, WIDTH), half),
            pltpu.VMEM((PAIRS * ROWS, ROWS * CAPS), half),
            pltpu.VMEM((direct, PAIRS, ROWS, WIDTH), half),
            arrived,
            arrived,
            arrived,
            arrived,
            pltpu.VMEM((SLOTS, WIDTH), half),
            pltpu.VMEM((ORB, ORB, SLOTS), half),
            pltpu.VMEM((PB, 64, 64), jnp.float32),
            pltpu.VMEM((1024, 1024), half),
            pltpu.VMEM((256, 256), half),
            pltpu.VMEM((SLOTS, 2 * SLOTS), half),
            pltpu.VMEM((SLOTS, 2 * SLOTS), half),
            pltpu.VMEM((4, 1024, SLOTS), jnp.float32),
            pltpu.VMEM((ORB, ORB, SLOTS), half),
            pltpu.VMEM((SLOTS, SLOTS), jnp.float32),
            pltpu.VMEM((2 * MOST, MOST, 16, 128), half),
            pltpu.VMEM((PAIRS, MOST, 16, 128), half),
            pltpu.VMEM((PAIRS + 1, MOST, 16, 128), half),
            block,
            block,
            block,
            block,
            pltpu.SMEM((2, CAPS * PB), jnp.int32),
            dma((direct,)),
            dma,
            dma((direct, PAIRS)),
            dma((direct, PAIRS)),
            dma((2, STEPS, CHUNKS)),
            dma((2, STEPS, CHUNKS)),
            dma((PAIRS,)),
            dma((PAIRS,)),
            dma((TIMES,)),
            dma((TIMES,)),
            dma((TIMES,)),
            dma((TIMES,)),
        ],
        compiler_params=pltpu.CompilerParams(collective_id=0, has_side_effects=True),
        name="polarizability",
    )(
        pair_lists.T, cosine_weights, integrals.reshape(ROWS * CAPS, PB * WIDTH), coulomb_blocks,
        occ_density[0, 0], virt_density[0, 0],
    )


def solution(mesh):
    in_specs = (
        P("tensor", None, None),
        P(),
        P("tm", "tensor", None, None),
        P("tm", "tensor", None, None),
        P(),
        P(),
    )
    return jax.shard_map(
        per_device, mesh=mesh, in_specs=in_specs, out_specs=P("tm", "tensor", None), check_vma=False
    )
```

```python
import jax
import jax.numpy as jnp
from jax import lax
from jax.experimental import pallas as pl
from jax.experimental.pallas import tpu as pltpu
from jax.sharding import PartitionSpec as P

MESH = pl.DeviceIdType.MESH
MOST = 6
PB = 16
CAPS = 8
ORB = 64
ROWS = 32
PAIRS = 32
TIMES = 16
WIDTH = 256
SLOTS = MOST * 64
HALF = 128
STEPS = 6
NT = (((1,), (1,)), ((), ()))
TN = (((0,), (0,)), ((), ()))
ORDER = (0, 1, -1, 2, -2, 3, -3, 8, 4, -4, 7, 5, -5, -7, 6, -6)
PLACE = {distance: place for place, distance in enumerate(ORDER)}
DIRECT = (0, 8, 7, -7)


def iota(shape, axis):
    return lax.broadcasted_iota(jnp.int32, shape, axis)


def one_hot(mask):
    return mask.astype(jnp.float32).astype(jnp.bfloat16)


def mul(a, b, dims=None):
    if dims is None:
        return jnp.dot(a, b, preferred_element_type=jnp.float32)
    return lax.dot_general(a, b, dims, preferred_element_type=jnp.float32)


def low(x):
    return x.astype(jnp.bfloat16)


def kernel(
    lists_ref, cos_ref, rows_ref, factor_ref, occ_ref, virt_ref, out_ref,
    mine, route, early, stage, near0, near1, got1, got2, got3, tiles, factor, ko, kv, wide, part, half, mixed,
    gram, folded, terms, inbox, chi, times, spread, freqs, places,
    load_sem, factor_sem, send0, recv0, send1, recv1, sendz, recvz, send2, recv2, send3, recv3, send4, recv4,
):
    z = lax.axis_index("tm")
    me = lax.axis_index("tensor")
    got = (None, got1, got2, got3)
    near = (near0, near1)
    block = lax.div(me, 2)
    first = pl.multiple_of(lax.rem(me, 2) * ROWS, ROWS)

    def at(distance):
        return lax.rem(z + distance + TIMES, TIMES)

    def load(e):
        columns = pl.ds(pl.multiple_of(at(DIRECT[e]) * WIDTH, WIDTH), WIDTH)
        return pltpu.make_async_copy(rows_ref.at[:, columns], mine.at[e], load_sem.at[e])

    for e in range(len(DIRECT)):
        load(e).start()
    fetch = pltpu.make_async_copy(factor_ref, factor, factor_sem)
    fetch.start()

    barrier = pltpu.get_barrier_semaphore()

    def greet(i, carry):
        peer = lax.rem(me + i, PAIRS)
        pl.semaphore_signal(barrier, inc=1, device_id={"tensor": peer}, device_id_type=MESH)
        return carry

    for distance in (2, -2, 1, -1):
        pl.semaphore_signal(barrier, inc=1, device_id={"tm": at(distance)}, device_id_type=MESH)
    lax.fori_loop(1, PAIRS, greet, 0)

    column = lax.rem(iota((1, WIDTH), 1), CAPS)
    names = jnp.full((1, WIDTH), -1, jnp.int32)
    for c in range(CAPS):
        names = jnp.where(column == c, lists_ref[c, block], names)
    shape = (ROWS, WIDTH)
    code = jnp.where(iota(shape, 0) == jnp.right_shift(iota(shape, 1), 3), names, -1)
    for k in range(PAIRS):
        route[ROWS * k : ROWS * k + ROWS] = one_hot(code == k)

    def pack(e):
        load(e).wait()
        return low(mul(route[...], mine[e])).reshape(PAIRS, ROWS, WIDTH)

    packed = pack(0)
    for c in range(2):
        early[c] = packed[:, :, HALF * c : HALF * c + HALF]
    pl.semaphore_wait(barrier, PAIRS + 3)

    def exchange(e, i):
        peer = lax.rem(me + i, PAIRS)
        if e < 2:
            src, dst, send, recv = early.at[e, peer], near[e], send0.at[e, i], recv0.at[e, i]
        else:
            src, dst = stage.at[e - 2, peer], got[e - 1]
            send, recv = send1.at[e - 2, i], recv1.at[e - 2, i]
        return pltpu.make_async_remote_copy(
            src_ref=src,
            dst_ref=dst.at[block, pl.ds(first, ROWS)],
            send_sem=send,
            recv_sem=recv,
            device_id={"tensor": peer},
            device_id_type=MESH,
        )

    def send_rows(e):
        def start(i, carry):
            exchange(e, i).start()
            return carry

        lax.fori_loop(1, PAIRS, start, 0)

    send_rows(0)
    send_rows(1)

    members, ranks, count = [], [], jnp.int32(0)
    for p in range(PB):
        named = lists_ref[0, p] == me
        for c in range(1, CAPS):
            named = named | (lists_ref[c, p] == me)
        members.append(named)
        ranks.append(count)
        count = count + named.astype(jnp.int32)
    chosen = []
    for j in range(MOST):
        found = jnp.int32(PB)
        for p in range(PB):
            found = jnp.where(members[p] & (ranks[p] == j), p, found)
        chosen.append(found)
    slot_of = [jnp.where(members[p], jnp.minimum(ranks[p], MOST - 1), 0) for p in range(PB)]

    for c in range(2):
        near[c][PB] = jnp.zeros((64, HALF), jnp.bfloat16)
        near[c][block, pl.ds(first, ROWS)] = early[c, me]

    square = (ORB, ORB)
    held = jnp.right_shift(iota(square, 0), 2)
    owner = jnp.zeros(square, jnp.int32)
    for place, distance in enumerate(ORDER):
        owner = jnp.where(held == place, at(distance), owner)
    order = one_hot(iota(square, 1) == 4 * owner + jnp.bitwise_and(iota(square, 0), 3))
    occ = low(mul(low(mul(order, occ_ref[...])), order, NT))
    big = ORB * 16
    pick = one_hot(jnp.right_shift(iota((big, ORB), 0), 4) == iota((big, ORB), 1))
    full = mul(low(mul(pick, occ, NT)), pick, NT)
    same = jnp.bitwise_and(jnp.bitwise_xor(iota((big, big), 0), iota((big, big), 1)), 15) == 0
    ko[...] = low(jnp.where(same, full, 0.0))
    pick = one_hot(jnp.bitwise_and(iota((HALF, ORB), 0), ORB - 1) == iota((HALF, ORB), 1))
    full = mul(low(mul(pick, virt_ref[...], NT)), pick, NT)
    same = jnp.bitwise_xor(iota((HALF, HALF), 0), iota((HALF, HALF), 1)) < ORB
    kv[...] = low(jnp.where(same, full, 0.0))
    for e in range(1, len(DIRECT)):
        stage[e - 1] = pack(e)
        got[e][PB] = jnp.zeros((64, WIDTH), jnp.bfloat16)
        got[e][block, pl.ds(first, ROWS)] = stage[e - 1, me]

    def finish_rows(e):
        def finish(i, carry):
            exchange(e, i).wait()
            return carry

        lax.fori_loop(1, PAIRS, finish, 0)

    def take_half(c):
        finish_rows(c)
        for j in range(MOST):
            tiles[0, c, 64 * j : 64 * j + 64] = near[c][chosen[j]]

    def take_rows(e):
        finish_rows(e + 1)
        place = PLACE[DIRECT[e]]
        for j in range(MOST):
            rows = got[e][chosen[j]]
            for c in range(2):
                tiles[place, c, 64 * j : 64 * j + 64] = rows[:, HALF * c : HALF * c + HALF]
        virtual(place)

    def virtual(place):
        for c in range(2):
            value = low(mul(kv[...], tiles[place, c], NT)).reshape(2, ORB, SLOTS)
            half[4 * place + 2 * c : 4 * place + 2 * c + 2] = value

    def virtuals(distance):
        virtual(PLACE[distance])
        virtual(PLACE[-distance])

    def hop(way, step, chunk):
        sign = -1 if way == 0 else 1
        return pltpu.make_async_remote_copy(
            src_ref=tiles.at[PLACE[sign * (step - 1)], chunk],
            dst_ref=tiles.at[PLACE[sign * step], chunk],
            send_sem=sendz.at[way, step - 1, chunk],
            recv_sem=recvz.at[way, step - 1, chunk],
            device_id={"tm": at(-sign)},
            device_id_type=MESH,
        )

    def contract(b, g0, g1):
        def one(g, carry):
            nus = pl.ds(pl.multiple_of(g * 16, 16), 16)
            x = half[16 * b : 16 * b + 16, nus, :].reshape(WIDTH, SLOTS)
            y = mul(ko[:, WIDTH * b : WIDTH * b + WIDTH], x)
            if b == 0:
                part[g] = y
            elif b < 3:
                part[g] += y
            else:
                mixed[:, nus, :] = low(part[g] + y).reshape(ORB, 16, SLOTS)
            return carry

        lax.fori_loop(g0, g1, one, 0)

    def factors():
        fetch.wait()
        wide[...] = jnp.zeros_like(wide)
        shape = (ORB, 2 * ORB)
        ahead = one_hot(iota(shape, 0) == iota(shape, 1))
        behind = one_hot(iota(shape, 0) + ORB == iota(shape, 1))
        for j in range(MOST):
            value = low(factor[jnp.minimum(chosen[j], PB - 1)])
            m, n = j // 2, j % 2
            wide[m, 64 * n : 64 * n + 64, 128 * n : 128 * n + 128] = low(mul(value, ahead))
            lanes = slice(256 + 128 * n, 384 + 128 * n)
            wide[m, 64 * n : 64 * n + 64, lanes] = low(mul(value, behind))

    under = {
        (1, 0): (),
        (1, 1): (factors, lambda: virtual(0)),
        (2, 1): (lambda: virtuals(1),),
        (3, 1): (lambda: virtuals(2), lambda: contract(0, 0, 2)),
        (4, 0): (lambda: contract(0, 2, 4),),
        (4, 1): (lambda: virtuals(3), lambda: take_rows(1)),
        (5, 0): (lambda: contract(1, 0, 2),),
        (5, 1): (lambda: virtuals(4), lambda: contract(1, 2, 4)),
        (6, 0): (lambda: take_rows(2),),
        (6, 1): (lambda: virtuals(5), lambda: contract(2, 0, 4)),
    }
    for step in range(1, STEPS + 1):
        for chunk in range(2):
            if step == 1:
                take_half(chunk)
            for way in range(2):
                if step > 1:
                    hop(way, step - 1, chunk).wait_recv()
                hop(way, step, chunk).start()
            if step == 1 and chunk == 1:
                for e in range(1, len(DIRECT)):
                    send_rows(e + 1)
            for work in under.get((step, chunk), ()):
                work()
    take_rows(3)
    for chunk in range(2):
        for way in range(2):
            hop(way, STEPS, chunk).wait_recv()
    virtuals(STEPS)
    contract(3, 0, 4)
    gram[...] = jnp.zeros_like(gram)

    def overlap(b, carry):
        rows = jnp.concatenate([tiles[4 * b + i, c] for i in range(4) for c in range(2)], axis=1)
        gram[...] += mul(rows, mixed[pl.ds(16 * b, 16)].reshape(4 * WIDTH, SLOTS))
        return carry

    lax.fori_loop(0, 4, overlap, 0)
    term = low(jnp.transpose(gram[...]))
    for m in range(MOST // 2):
        value = mul(term[:, 128 * m : 128 * m + 128], wide[m])
        for b in range(2 * MOST):
            upper, lower = value[32 * b : 32 * b + 16], value[32 * b + 16 : 32 * b + 32]
            for n in range(2):
                lanes = slice(128 * n, 128 * n + 128)
                after = slice(256 + 128 * n, 384 + 128 * n)
                folded[b, 2 * m + n] = low(upper[:, lanes] + lower[:, after])
    for d in range(PAIRS):
        terms[d] = folded[slot_of[d // 2] * 2 + d % 2]

    def trade(axis, count, src, dst, send, recv):
        here = lax.axis_index(axis)

        def one(i):
            peer = lax.rem(here + i, count)
            return pltpu.make_async_remote_copy(
                src_ref=src.at[peer],
                dst_ref=dst.at[here],
                send_sem=send.at[i],
                recv_sem=recv.at[i],
                device_id={axis: peer},
                device_id_type=MESH,
            )

        def begin(i, carry):
            one(i).start()
            return carry

        def end(i, carry):
            one(i).wait()
            return carry

        lax.fori_loop(1, count, begin, 0)
        dst[here] = src[here]
        return lambda: lax.fori_loop(1, count, end, 0)

    arrive = trade("tensor", PAIRS, terms, inbox, send2, recv2)
    inbox[PAIRS, 0] = jnp.zeros((16, 128), jnp.bfloat16)

    def locate(c, carry):
        name = lists_ref[c, block]
        rank = jnp.int32(0)
        for q in range(PB):
            named = lists_ref[0, q] == name
            for other in range(1, CAPS):
                named = named | (lists_ref[other, q] == name)
            places[0, c * PB + q] = jnp.where(named, name, PAIRS)
            places[1, c * PB + q] = jnp.where(named, jnp.minimum(rank, MOST - 1), 0)
            rank = rank + named.astype(jnp.int32)
        return carry

    lax.fori_loop(0, CAPS, locate, 0)
    for step in range(1, STEPS + 1):
        for chunk in range(2):
            for way in range(2):
                hop(way, step, chunk).wait_send()
    arrive()
    for q in range(PB):
        total = inbox[places[0, q], places[1, q]].astype(jnp.float32)
        for c in range(1, CAPS):
            spot = c * PB + q
            total += inbox[places[0, spot], places[1, spot]].astype(jnp.float32)
        chi[q] = low(total)

    trade("tm", TIMES, chi, times, send3, recv3)()
    series = [times[t].astype(jnp.float32) for t in range(TIMES)]
    for f in range(TIMES):
        total = cos_ref[f, 0] * series[0]
        for t in range(1, TIMES):
            total += cos_ref[f, t] * series[t]
        spread[f] = low(total)
    trade("tm", TIMES, spread, freqs, send4, recv4)()

    out_ref[...] = freqs[...]


def unfold_kernel(freqs_ref, out_ref):
    first = iota((16, 128), 1) < 64
    for m in range(PB // 2):
        even = freqs_ref[2 * m].astype(jnp.float32)
        odd = freqs_ref[2 * m + 1].astype(jnp.float32)
        lanes = slice(128 * m, 128 * m + 128)
        out_ref[0, 0:16, lanes] = jnp.where(first, even, pltpu.roll(odd, 64, 1))
        out_ref[0, 16:32, lanes] = jnp.where(first, pltpu.roll(even, 64, 1), odd)


def per_device(integrals, pair_lists, occ_density, virt_density, cosine_weights, coulomb_blocks):
    smem = pl.BlockSpec(memory_space=pltpu.SMEM)
    vmem = pl.BlockSpec(memory_space=pltpu.VMEM)
    hbm = pl.BlockSpec(memory_space=pl.ANY)
    dma = pltpu.SemaphoreType.DMA
    half = jnp.bfloat16
    direct = len(DIRECT)
    block = pltpu.VMEM((PB, 16, 128), half)
    near = pltpu.VMEM((PB + 1, 64, HALF), half)
    arrived = pltpu.VMEM((PB + 1, 64, WIDTH), half)
    freqs = pl.pallas_call(
        kernel,
        out_shape=jax.ShapeDtypeStruct((PB, 16, 128), half),
        in_specs=[smem, smem, hbm, hbm, vmem, vmem],
        out_specs=vmem,
        scratch_shapes=[
            pltpu.VMEM((direct, ROWS * CAPS, WIDTH), half),
            pltpu.VMEM((PAIRS * ROWS, ROWS * CAPS), half),
            pltpu.VMEM((2, PAIRS, ROWS, HALF), half),
            pltpu.VMEM((direct - 1, PAIRS, ROWS, WIDTH), half),
            near,
            near,
            arrived,
            arrived,
            arrived,
            pltpu.VMEM((TIMES, 2, SLOTS, HALF), half),
            pltpu.VMEM((PB, 64, 64), jnp.float32),
            pltpu.VMEM((1024, 1024), half),
            pltpu.VMEM((HALF, HALF), half),
            pltpu.VMEM((MOST // 2, 128, 512), half),
            pltpu.VMEM((4, 1024, SLOTS), jnp.float32),
            pltpu.VMEM((ORB, ORB, SLOTS), half),
            pltpu.VMEM((ORB, ORB, SLOTS), half),
            pltpu.VMEM((SLOTS, SLOTS), jnp.float32),
            pltpu.VMEM((2 * MOST, MOST, 16, 128), half),
            pltpu.VMEM((PAIRS, MOST, 16, 128), half),
            pltpu.VMEM((PAIRS + 1, MOST, 16, 128), half),
            block,
            block,
            block,
            block,
            pltpu.SMEM((2, CAPS * PB), jnp.int32),
            dma((direct,)),
            dma,
            dma((2, PAIRS)),
            dma((2, PAIRS)),
            dma((direct - 1, PAIRS)),
            dma((direct - 1, PAIRS)),
            dma((2, STEPS, 2)),
            dma((2, STEPS, 2)),
            dma((PAIRS,)),
            dma((PAIRS,)),
            dma((TIMES,)),
            dma((TIMES,)),
            dma((TIMES,)),
            dma((TIMES,)),
        ],
        compiler_params=pltpu.CompilerParams(collective_id=0, has_side_effects=True),
        name="polarizability",
    )(
        pair_lists.T, cosine_weights, integrals.reshape(ROWS * CAPS, PB * WIDTH), coulomb_blocks,
        occ_density[0, 0], virt_density[0, 0],
    )
    return pl.pallas_call(
        unfold_kernel,
        out_shape=jax.ShapeDtypeStruct((1, ROWS, PB * 64), jnp.float32),
        in_specs=[vmem],
        out_specs=vmem,
        name="unfold",
    )(freqs)


def solution(mesh):
    in_specs = (
        P("tensor", None, None),
        P(),
        P("tm", "tensor", None, None),
        P("tm", "tensor", None, None),
        P(),
        P(),
    )
    return jax.shard_map(
        per_device, mesh=mesh, in_specs=in_specs, out_specs=P("tm", "tensor", None), check_vma=False
    )
```

```python
import jax
import jax.numpy as jnp
from jax import lax
from jax.experimental import pallas as pl
from jax.experimental.pallas import tpu as pltpu
from jax.sharding import PartitionSpec as P

MESH = pl.DeviceIdType.MESH
MOST = 6
PB = 16
CAPS = 8
ORB = 64
ROWS = 32
PAIRS = 32
TIMES = 16
WIDTH = 256
SLOTS = MOST * 64
HALF = 128
STEPS = 6
NT = (((1,), (1,)), ((), ()))
TN = (((0,), (0,)), ((), ()))
ORDER = (0, 1, -1, 2, -2, 3, -3, 8, 4, -4, 7, 5, -5, -7, 6, -6)
PLACE = {distance: place for place, distance in enumerate(ORDER)}
DIRECT = (0, 8, 7, -7)


def iota(shape, axis):
    return lax.broadcasted_iota(jnp.int32, shape, axis)


def one_hot(mask):
    return mask.astype(jnp.float32).astype(jnp.bfloat16)


def mul(a, b, dims=None):
    if dims is None:
        return jnp.dot(a, b, preferred_element_type=jnp.float32)
    return lax.dot_general(a, b, dims, preferred_element_type=jnp.float32)


def low(x):
    return x.astype(jnp.bfloat16)


def kernel(
    lists_ref, cos_ref, rows_ref, factor_ref, occ_ref, virt_ref, out_ref,
    mine, route, early, stage, near0, near1, got1, got2, got3, tiles, factor, ko, kv, wide, part, half, mixed,
    folded, terms, inbox, chi, times, spread, freqs, places,
    load_sem, factor_sem, send0, recv0, send1, recv1, sendz, recvz, send2, recv2, send3, recv3, send4, recv4,
):
    z = lax.axis_index("tm")
    me = lax.axis_index("tensor")
    got = (None, got1, got2, got3)
    near = (near0, near1)
    block = lax.div(me, 2)
    first = pl.multiple_of(lax.rem(me, 2) * ROWS, ROWS)

    def at(distance):
        return lax.rem(z + distance + TIMES, TIMES)

    def load(e):
        columns = pl.ds(pl.multiple_of(at(DIRECT[e]) * WIDTH, WIDTH), WIDTH)
        return pltpu.make_async_copy(rows_ref.at[:, columns], mine.at[e], load_sem.at[e])

    for e in range(len(DIRECT)):
        load(e).start()
    fetch = pltpu.make_async_copy(factor_ref, factor, factor_sem)
    fetch.start()

    barrier = pltpu.get_barrier_semaphore()

    def greet(i, carry):
        peer = lax.rem(me + i, PAIRS)
        pl.semaphore_signal(barrier, inc=1, device_id={"tensor": peer}, device_id_type=MESH)
        return carry

    for distance in (2, -2, 1, -1):
        pl.semaphore_signal(barrier, inc=1, device_id={"tm": at(distance)}, device_id_type=MESH)
    lax.fori_loop(1, PAIRS, greet, 0)

    column = lax.rem(iota((1, WIDTH), 1), CAPS)
    names = jnp.full((1, WIDTH), -1, jnp.int32)
    for c in range(CAPS):
        names = jnp.where(column == c, lists_ref[c, block], names)
    shape = (ROWS, WIDTH)
    code = jnp.where(iota(shape, 0) == jnp.right_shift(iota(shape, 1), 3), names, -1)
    for k in range(PAIRS):
        route[ROWS * k : ROWS * k + ROWS] = one_hot(code == k)

    def pack(e):
        load(e).wait()
        return low(mul(route[...], mine[e])).reshape(PAIRS, ROWS, WIDTH)

    def pack_half(c):
        part_rows = mine[0, :, HALF * c : HALF * c + HALF]
        early[c] = low(mul(route[...], part_rows)).reshape(PAIRS, ROWS, HALF)

    load(0).wait()
    pack_half(0)
    pl.semaphore_wait(barrier, PAIRS + 3)

    def exchange(e, i):
        peer = lax.rem(me + i, PAIRS)
        if e < 2:
            src, dst, send, recv = early.at[e, peer], near[e], send0.at[e, i], recv0.at[e, i]
        else:
            src, dst = stage.at[e - 2, peer], got[e - 1]
            send, recv = send1.at[e - 2, i], recv1.at[e - 2, i]
        return pltpu.make_async_remote_copy(
            src_ref=src,
            dst_ref=dst.at[block, pl.ds(first, ROWS)],
            send_sem=send,
            recv_sem=recv,
            device_id={"tensor": peer},
            device_id_type=MESH,
        )

    def send_rows(e):
        def start(i, carry):
            exchange(e, i).start()
            return carry

        lax.fori_loop(1, PAIRS, start, 0)

    send_rows(0)
    pack_half(1)
    send_rows(1)

    members, ranks, count = [], [], jnp.int32(0)
    for p in range(PB):
        named = lists_ref[0, p] == me
        for c in range(1, CAPS):
            named = named | (lists_ref[c, p] == me)
        members.append(named)
        ranks.append(count)
        count = count + named.astype(jnp.int32)
    chosen = []
    for j in range(MOST):
        found = jnp.int32(PB)
        for p in range(PB):
            found = jnp.where(members[p] & (ranks[p] == j), p, found)
        chosen.append(found)
    slot_of = [jnp.where(members[p], jnp.minimum(ranks[p], MOST - 1), 0) for p in range(PB)]

    for c in range(2):
        near[c][PB] = jnp.zeros((64, HALF), jnp.bfloat16)
        near[c][block, pl.ds(first, ROWS)] = early[c, me]

    square = (ORB, ORB)
    held = jnp.right_shift(iota(square, 0), 2)
    owner = jnp.zeros(square, jnp.int32)
    for place, distance in enumerate(ORDER):
        owner = jnp.where(held == place, at(distance), owner)
    order = one_hot(iota(square, 1) == 4 * owner + jnp.bitwise_and(iota(square, 0), 3))
    occ = low(mul(low(mul(order, occ_ref[...])), order, NT))
    big = ORB * 16

    def spread_occ(b):
        pick = one_hot(jnp.right_shift(iota((big, ORB), 0), 4) == iota((big, ORB), 1))
        rows = low(mul(pick, occ, NT))
        full = mul(rows, pick[WIDTH * b : WIDTH * b + WIDTH], NT)
        shape = (big, WIDTH)
        same = jnp.bitwise_and(jnp.bitwise_xor(iota(shape, 0), iota(shape, 1)), 15) == 0
        ko[:, WIDTH * b : WIDTH * b + WIDTH] = low(jnp.where(same, full, 0.0))

    pick = one_hot(jnp.bitwise_and(iota((HALF, ORB), 0), ORB - 1) == iota((HALF, ORB), 1))
    full = mul(low(mul(pick, virt_ref[...], NT)), pick, NT)
    same = jnp.bitwise_xor(iota((HALF, HALF), 0), iota((HALF, HALF), 1)) < ORB
    kv[...] = low(jnp.where(same, full, 0.0))
    def prepare_rows(e):
        stage[e - 1] = pack(e)
        got[e][PB] = jnp.zeros((64, WIDTH), jnp.bfloat16)
        got[e][block, pl.ds(first, ROWS)] = stage[e - 1, me]

    def finish_rows(e):
        def finish(i, carry):
            exchange(e, i).wait()
            return carry

        lax.fori_loop(1, PAIRS, finish, 0)

    def take_half(c):
        finish_rows(c)
        for j in range(MOST):
            tiles[0, c, 64 * j : 64 * j + 64] = near[c][chosen[j]]

    def take_rows(e):
        finish_rows(e + 1)
        place = PLACE[DIRECT[e]]
        for j in range(MOST):
            rows = got[e][chosen[j]]
            for c in range(2):
                tiles[place, c, 64 * j : 64 * j + 64] = rows[:, HALF * c : HALF * c + HALF]
        virtual(place)

    def virtual(place):
        for c in range(2):
            value = low(mul(kv[...], tiles[place, c], NT)).reshape(2, ORB, SLOTS)
            half[4 * place + 2 * c : 4 * place + 2 * c + 2] = value

    def virtuals(distance):
        virtual(PLACE[distance])
        virtual(PLACE[-distance])

    def hop(way, step, chunk):
        sign = -1 if way == 0 else 1
        return pltpu.make_async_remote_copy(
            src_ref=tiles.at[PLACE[sign * (step - 1)], chunk],
            dst_ref=tiles.at[PLACE[sign * step], chunk],
            send_sem=sendz.at[way, step - 1, chunk],
            recv_sem=recvz.at[way, step - 1, chunk],
            device_id={"tm": at(-sign)},
            device_id_type=MESH,
        )

    def contract(b, g0, g1):
        def one(g, carry):
            nus = pl.ds(pl.multiple_of(g * 16, 16), 16)
            x = half[16 * b : 16 * b + 16, nus, :].reshape(WIDTH, SLOTS)
            y = mul(ko[:, WIDTH * b : WIDTH * b + WIDTH], x)
            if b == 0:
                part[g] = y
            elif b < 3:
                part[g] += y
            else:
                mixed[:, nus, :] = low(part[g] + y).reshape(ORB, 16, SLOTS)
            return carry

        lax.fori_loop(g0, g1, one, 0)

    def factors():
        fetch.wait()
        wide[...] = jnp.zeros_like(wide)
        shape = (ORB, 2 * ORB)
        ahead = one_hot(iota(shape, 0) == iota(shape, 1))
        behind = one_hot(iota(shape, 0) + ORB == iota(shape, 1))
        for j in range(MOST):
            value = low(factor[jnp.minimum(chosen[j], PB - 1)])
            m, n = j // 2, j % 2
            wide[m, 64 * n : 64 * n + 64, 128 * n : 128 * n + 128] = low(mul(value, ahead))
            lanes = slice(256 + 128 * n, 384 + 128 * n)
            wide[m, 64 * n : 64 * n + 64, lanes] = low(mul(value, behind))

    def send_later(e):
        prepare_rows(e)
        send_rows(e + 1)

    under = {
        (1, 1): (
            lambda: send_later(1),
            lambda: send_later(2),
            lambda: send_later(3),
            lambda: virtual(0),
        ),
        (2, 0): (lambda: spread_occ(0),),
        (2, 1): (lambda: virtuals(1), lambda: spread_occ(1)),
        (3, 0): (factors,),
        (3, 1): (lambda: virtuals(2), lambda: contract(0, 0, 2)),
        (4, 0): (lambda: contract(0, 2, 4),),
        (4, 1): (lambda: virtuals(3), lambda: take_rows(1)),
        (5, 0): (lambda: contract(1, 0, 2),),
        (5, 1): (lambda: virtuals(4), lambda: contract(1, 2, 4)),
        (6, 0): (lambda: take_rows(2), lambda: spread_occ(2)),
        (6, 1): (lambda: virtuals(5), lambda: contract(2, 0, 4), lambda: spread_occ(3)),
    }
    for step in range(1, STEPS + 1):
        for chunk in range(2):
            if step == 1:
                take_half(chunk)
            for way in range(2):
                if step > 1:
                    hop(way, step - 1, chunk).wait_recv()
                hop(way, step, chunk).start()
            for work in under.get((step, chunk), ()):
                work()
    take_rows(3)
    for chunk in range(2):
        for way in range(2):
            hop(way, STEPS, chunk).wait_recv()
    virtuals(STEPS)
    contract(3, 0, 4)
    rows = jnp.concatenate([tiles[i, c] for i in range(TIMES) for c in range(2)], axis=1)
    gram = mul(rows, mixed[...].reshape(TIMES * WIDTH, SLOTS))
    term = low(jnp.transpose(gram))
    for m in range(MOST // 2):
        value = mul(term[:, 128 * m : 128 * m + 128], wide[m])
        for b in range(2 * MOST):
            upper, lower = value[32 * b : 32 * b + 16], value[32 * b + 16 : 32 * b + 32]
            for n in range(2):
                lanes = slice(128 * n, 128 * n + 128)
                after = slice(256 + 128 * n, 384 + 128 * n)
                folded[b, 2 * m + n] = low(upper[:, lanes] + lower[:, after])
    for d in range(PAIRS):
        terms[d] = folded[slot_of[d // 2] * 2 + d % 2]

    def trade(axis, count, src, dst, send, recv):
        here = lax.axis_index(axis)

        def one(i):
            peer = lax.rem(here + i, count)
            return pltpu.make_async_remote_copy(
                src_ref=src.at[peer],
                dst_ref=dst.at[here],
                send_sem=send.at[i],
                recv_sem=recv.at[i],
                device_id={axis: peer},
                device_id_type=MESH,
            )

        def begin(i, carry):
            one(i).start()
            return carry

        def end(i, carry):
            one(i).wait()
            return carry

        lax.fori_loop(1, count, begin, 0)
        dst[here] = src[here]
        return lambda: lax.fori_loop(1, count, end, 0)

    arrive = trade("tensor", PAIRS, terms, inbox, send2, recv2)
    inbox[PAIRS, 0] = jnp.zeros((16, 128), jnp.bfloat16)

    def locate(c, carry):
        name = lists_ref[c, block]
        rank = jnp.int32(0)
        for q in range(PB):
            named = lists_ref[0, q] == name
            for other in range(1, CAPS):
                named = named | (lists_ref[other, q] == name)
            places[0, c * PB + q] = jnp.where(named, name, PAIRS)
            places[1, c * PB + q] = jnp.where(named, jnp.minimum(rank, MOST - 1), 0)
            rank = rank + named.astype(jnp.int32)
        return carry

    lax.fori_loop(0, CAPS, locate, 0)
    for step in range(1, STEPS + 1):
        for chunk in range(2):
            for way in range(2):
                hop(way, step, chunk).wait_send()
    arrive()
    for q in range(PB):
        total = inbox[places[0, q], places[1, q]].astype(jnp.float32)
        for c in range(1, CAPS):
            spot = c * PB + q
            total += inbox[places[0, spot], places[1, spot]].astype(jnp.float32)
        chi[q] = low(total)

    trade("tm", TIMES, chi, times, send3, recv3)()
    series = [times[t].astype(jnp.float32) for t in range(TIMES)]
    for f in range(TIMES):
        total = cos_ref[f, 0] * series[0]
        for t in range(1, TIMES):
            total += cos_ref[f, t] * series[t]
        spread[f] = low(total)
    trade("tm", TIMES, spread, freqs, send4, recv4)()

    out_ref[...] = freqs[...]


def unfold_kernel(freqs_ref, out_ref):
    first = iota((16, 128), 1) < 64
    for m in range(PB // 2):
        even = freqs_ref[2 * m].astype(jnp.float32)
        odd = freqs_ref[2 * m + 1].astype(jnp.float32)
        lanes = slice(128 * m, 128 * m + 128)
        out_ref[0, 0:16, lanes] = jnp.where(first, even, pltpu.roll(odd, 64, 1))
        out_ref[0, 16:32, lanes] = jnp.where(first, pltpu.roll(even, 64, 1), odd)


def per_device(integrals, pair_lists, occ_density, virt_density, cosine_weights, coulomb_blocks):
    smem = pl.BlockSpec(memory_space=pltpu.SMEM)
    vmem = pl.BlockSpec(memory_space=pltpu.VMEM)
    hbm = pl.BlockSpec(memory_space=pl.ANY)
    dma = pltpu.SemaphoreType.DMA
    half = jnp.bfloat16
    direct = len(DIRECT)
    block = pltpu.VMEM((PB, 16, 128), half)
    near = pltpu.VMEM((PB + 1, 64, HALF), half)
    arrived = pltpu.VMEM((PB + 1, 64, WIDTH), half)
    freqs = pl.pallas_call(
        kernel,
        out_shape=jax.ShapeDtypeStruct((PB, 16, 128), half),
        in_specs=[smem, smem, hbm, hbm, vmem, vmem],
        out_specs=vmem,
        scratch_shapes=[
            pltpu.VMEM((direct, ROWS * CAPS, WIDTH), half),
            pltpu.VMEM((PAIRS * ROWS, ROWS * CAPS), half),
            pltpu.VMEM((2, PAIRS, ROWS, HALF), half),
            pltpu.VMEM((direct - 1, PAIRS, ROWS, WIDTH), half),
            near,
            near,
            arrived,
            arrived,
            arrived,
            pltpu.VMEM((TIMES, 2, SLOTS, HALF), half),
            pltpu.VMEM((PB, 64, 64), jnp.float32),
            pltpu.VMEM((1024, 1024), half),
            pltpu.VMEM((HALF, HALF), half),
            pltpu.VMEM((MOST // 2, 128, 512), half),
            pltpu.VMEM((4, 1024, SLOTS), jnp.float32),
            pltpu.VMEM((ORB, ORB, SLOTS), half),
            pltpu.VMEM((ORB, ORB, SLOTS), half),
            pltpu.VMEM((2 * MOST, MOST, 16, 128), half),
            pltpu.VMEM((PAIRS, MOST, 16, 128), half),
            pltpu.VMEM((PAIRS + 1, MOST, 16, 128), half),
            block,
            block,
            block,
            block,
            pltpu.SMEM((2, CAPS * PB), jnp.int32),
            dma((direct,)),
            dma,
            dma((2, PAIRS)),
            dma((2, PAIRS)),
            dma((direct - 1, PAIRS)),
            dma((direct - 1, PAIRS)),
            dma((2, STEPS, 2)),
            dma((2, STEPS, 2)),
            dma((PAIRS,)),
            dma((PAIRS,)),
            dma((TIMES,)),
            dma((TIMES,)),
            dma((TIMES,)),
            dma((TIMES,)),
        ],
        compiler_params=pltpu.CompilerParams(collective_id=0, has_side_effects=True),
        name="polarizability",
    )(
        pair_lists.T, cosine_weights, integrals.reshape(ROWS * CAPS, PB * WIDTH), coulomb_blocks,
        occ_density[0, 0], virt_density[0, 0],
    )
    return pl.pallas_call(
        unfold_kernel,
        out_shape=jax.ShapeDtypeStruct((1, ROWS, PB * 64), jnp.float32),
        in_specs=[vmem],
        out_specs=vmem,
        name="unfold",
    )(freqs)


def solution(mesh):
    in_specs = (
        P("tensor", None, None),
        P(),
        P("tm", "tensor", None, None),
        P("tm", "tensor", None, None),
        P(),
        P(),
    )
    return jax.shard_map(
        per_device, mesh=mesh, in_specs=in_specs, out_specs=P("tm", "tensor", None), check_vma=False
    )
```

```python
import jax
import jax.numpy as jnp
from jax import lax
from jax.experimental import pallas as pl
from jax.experimental.pallas import tpu as pltpu
from jax.sharding import PartitionSpec as P

MESH = pl.DeviceIdType.MESH
MOST = 6
PB = 16
CAPS = 8
ORB = 64
ROWS = 32
PAIRS = 32
TIMES = 16
WIDTH = 256
SLOTS = MOST * 64
HALF = 128
STEPS = 6
NT = (((1,), (1,)), ((), ()))
TN = (((0,), (0,)), ((), ()))
ORDER = (0, 1, -1, 2, -2, 3, -3, 8, 4, -4, 7, 5, -5, -7, 6, -6)
PLACE = {distance: place for place, distance in enumerate(ORDER)}
DIRECT = (0, 8, 7, -7)


def iota(shape, axis):
    return lax.broadcasted_iota(jnp.int32, shape, axis)


def one_hot(mask):
    return mask.astype(jnp.float32).astype(jnp.bfloat16)


def mul(a, b, dims=None):
    if dims is None:
        return jnp.dot(a, b, preferred_element_type=jnp.float32)
    return lax.dot_general(a, b, dims, preferred_element_type=jnp.float32)


def low(x):
    return x.astype(jnp.bfloat16)


def kernel(
    lists_ref, cos_ref, rows_ref, factor_ref, occ_ref, virt_ref, out_ref,
    mine, route, early, stage, near0, near1, got1, got2, got3, tiles, factor, ko, kv, wide, part, half, mixed,
    folded, terms, inbox, chi, times, spread, freqs, waves, places,
    load_sem, factor_sem, send0, recv0, send1, recv1, sendz, recvz, send2, recv2, send3, recv3, send4, recv4,
):
    z = lax.axis_index("tm")
    me = lax.axis_index("tensor")
    got = (None, got1, got2, got3)
    near = (near0, near1)
    block = lax.div(me, 2)
    first = pl.multiple_of(lax.rem(me, 2) * ROWS, ROWS)

    def at(distance):
        return lax.rem(z + distance + TIMES, TIMES)

    def load(e):
        columns = pl.ds(pl.multiple_of(at(DIRECT[e]) * WIDTH, WIDTH), WIDTH)
        return pltpu.make_async_copy(rows_ref.at[:, columns], mine.at[e], load_sem.at[e])

    for e in range(len(DIRECT)):
        load(e).start()
    fetch = pltpu.make_async_copy(factor_ref, factor, factor_sem)
    fetch.start()

    barrier = pltpu.get_barrier_semaphore()

    def greet(i, carry):
        peer = lax.rem(me + i, PAIRS)
        pl.semaphore_signal(barrier, inc=1, device_id={"tensor": peer}, device_id_type=MESH)
        return carry

    for distance in (2, -2, 1, -1):
        pl.semaphore_signal(barrier, inc=1, device_id={"tm": at(distance)}, device_id_type=MESH)
    lax.fori_loop(1, PAIRS, greet, 0)

    column = lax.rem(iota((1, WIDTH), 1), CAPS)
    names = jnp.full((1, WIDTH), -1, jnp.int32)
    for c in range(CAPS):
        names = jnp.where(column == c, lists_ref[c, block], names)
    shape = (ROWS, WIDTH)
    code = jnp.where(iota(shape, 0) == jnp.right_shift(iota(shape, 1), 3), names, -1)
    for k in range(PAIRS):
        route[ROWS * k : ROWS * k + ROWS] = one_hot(code == k)

    def pack(e):
        load(e).wait()
        return low(mul(route[...], mine[e])).reshape(PAIRS, ROWS, WIDTH)

    def pack_half(c):
        part_rows = mine[0, :, HALF * c : HALF * c + HALF]
        early[c] = low(mul(route[...], part_rows)).reshape(PAIRS, ROWS, HALF)

    load(0).wait()
    pack_half(0)
    pl.semaphore_wait(barrier, PAIRS + 3)

    def exchange(e, i):
        peer = lax.rem(me + i, PAIRS)
        if e < 2:
            src, dst, send, recv = early.at[e, peer], near[e], send0.at[e, i], recv0.at[e, i]
        else:
            src, dst = stage.at[e - 2, peer], got[e - 1]
            send, recv = send1.at[e - 2, i], recv1.at[e - 2, i]
        return pltpu.make_async_remote_copy(
            src_ref=src,
            dst_ref=dst.at[block, pl.ds(first, ROWS)],
            send_sem=send,
            recv_sem=recv,
            device_id={"tensor": peer},
            device_id_type=MESH,
        )

    def send_rows(e):
        def start(i, carry):
            exchange(e, i).start()
            return carry

        lax.fori_loop(1, PAIRS, start, 0)

    send_rows(0)
    pack_half(1)
    send_rows(1)

    members, ranks, count = [], [], jnp.int32(0)
    for p in range(PB):
        named = lists_ref[0, p] == me
        for c in range(1, CAPS):
            named = named | (lists_ref[c, p] == me)
        members.append(named)
        ranks.append(count)
        count = count + named.astype(jnp.int32)
    chosen = []
    for j in range(MOST):
        found = jnp.int32(PB)
        for p in range(PB):
            found = jnp.where(members[p] & (ranks[p] == j), p, found)
        chosen.append(found)
    slot_of = [jnp.where(members[p], jnp.minimum(ranks[p], MOST - 1), 0) for p in range(PB)]

    for c in range(2):
        near[c][PB] = jnp.zeros((64, HALF), jnp.bfloat16)
        near[c][block, pl.ds(first, ROWS)] = early[c, me]

    square = (ORB, ORB)
    held = jnp.right_shift(iota(square, 0), 2)
    owner = jnp.zeros(square, jnp.int32)
    for place, distance in enumerate(ORDER):
        owner = jnp.where(held == place, at(distance), owner)
    order = one_hot(iota(square, 1) == 4 * owner + jnp.bitwise_and(iota(square, 0), 3))
    occ = low(mul(low(mul(order, occ_ref[...])), order, NT))
    big = ORB * 16

    def spread_occ(b):
        pick = one_hot(jnp.right_shift(iota((big, ORB), 0), 4) == iota((big, ORB), 1))
        rows = low(mul(pick, occ, NT))
        full = mul(rows, pick[WIDTH * b : WIDTH * b + WIDTH], NT)
        shape = (big, WIDTH)
        same = jnp.bitwise_and(jnp.bitwise_xor(iota(shape, 0), iota(shape, 1)), 15) == 0
        ko[:, WIDTH * b : WIDTH * b + WIDTH] = low(jnp.where(same, full, 0.0))

    pick = one_hot(jnp.bitwise_and(iota((HALF, ORB), 0), ORB - 1) == iota((HALF, ORB), 1))
    full = mul(low(mul(pick, virt_ref[...], NT)), pick, NT)
    same = jnp.bitwise_xor(iota((HALF, HALF), 0), iota((HALF, HALF), 1)) < ORB
    kv[...] = low(jnp.where(same, full, 0.0))
    def prepare_rows(e):
        stage[e - 1] = pack(e)
        got[e][PB] = jnp.zeros((64, WIDTH), jnp.bfloat16)
        got[e][block, pl.ds(first, ROWS)] = stage[e - 1, me]

    def finish_rows(e):
        def finish(i, carry):
            exchange(e, i).wait()
            return carry

        lax.fori_loop(1, PAIRS, finish, 0)

    def take_half(c):
        finish_rows(c)
        for j in range(MOST):
            tiles[0, c, 64 * j : 64 * j + 64] = near[c][chosen[j]]

    def take_rows(e):
        finish_rows(e + 1)
        place = PLACE[DIRECT[e]]
        for j in range(MOST):
            rows = got[e][chosen[j]]
            for c in range(2):
                tiles[place, c, 64 * j : 64 * j + 64] = rows[:, HALF * c : HALF * c + HALF]
        virtual(place)

    def virtual(place):
        for c in range(2):
            value = low(mul(kv[...], tiles[place, c], NT)).reshape(2, ORB, SLOTS)
            half[4 * place + 2 * c : 4 * place + 2 * c + 2] = value

    def virtuals(distance):
        virtual(PLACE[distance])
        virtual(PLACE[-distance])

    def hop(way, step, chunk):
        sign = -1 if way == 0 else 1
        return pltpu.make_async_remote_copy(
            src_ref=tiles.at[PLACE[sign * (step - 1)], chunk],
            dst_ref=tiles.at[PLACE[sign * step], chunk],
            send_sem=sendz.at[way, step - 1, chunk],
            recv_sem=recvz.at[way, step - 1, chunk],
            device_id={"tm": at(-sign)},
            device_id_type=MESH,
        )

    def contract(b, g0, g1):
        def one(g, carry):
            nus = pl.ds(pl.multiple_of(g * 16, 16), 16)
            x = half[16 * b : 16 * b + 16, nus, :].reshape(WIDTH, SLOTS)
            y = mul(ko[:, WIDTH * b : WIDTH * b + WIDTH], x)
            if b == 0:
                part[g] = y
            elif b < 3:
                part[g] += y
            else:
                mixed[:, nus, :] = low(part[g] + y).reshape(ORB, 16, SLOTS)
            return carry

        lax.fori_loop(g0, g1, one, 0)

    def factors():
        fetch.wait()
        wide[...] = jnp.zeros_like(wide)
        shape = (ORB, 2 * ORB)
        ahead = one_hot(iota(shape, 0) == iota(shape, 1))
        behind = one_hot(iota(shape, 0) + ORB == iota(shape, 1))
        for j in range(MOST):
            value = low(factor[jnp.minimum(chosen[j], PB - 1)])
            m, n = j // 2, j % 2
            wide[m, 64 * n : 64 * n + 64, 128 * n : 128 * n + 128] = low(mul(value, ahead))
            lanes = slice(256 + 128 * n, 384 + 128 * n)
            wide[m, 64 * n : 64 * n + 64, lanes] = low(mul(value, behind))

    def send_later(e):
        prepare_rows(e)
        send_rows(e + 1)

    def cosines():
        shape = (WIDTH, TIMES)
        pick = one_hot(jnp.right_shift(iota(shape, 0), 4) == iota(shape, 1))
        high = low(cos_ref[...])
        rest = low(cos_ref[...] - high.astype(jnp.float32))
        same = jnp.bitwise_xor(iota((WIDTH, WIDTH), 0), iota((WIDTH, WIDTH), 1))
        same = jnp.bitwise_and(same, 15) == 0
        for n, piece in enumerate((high, rest)):
            full = mul(low(mul(pick, piece)), pick, NT)
            waves[:, WIDTH * n : WIDTH * n + WIDTH] = low(jnp.where(same, full, 0.0))

    under = {
        (1, 1): (
            lambda: send_later(1),
            lambda: send_later(2),
            lambda: send_later(3),
            lambda: virtual(0),
        ),
        (2, 0): (lambda: spread_occ(0),),
        (2, 1): (lambda: virtuals(1), lambda: spread_occ(1)),
        (3, 0): (factors, cosines),
        (3, 1): (lambda: virtuals(2), lambda: contract(0, 0, 2)),
        (4, 0): (lambda: contract(0, 2, 4),),
        (4, 1): (lambda: virtuals(3), lambda: take_rows(1)),
        (5, 0): (lambda: contract(1, 0, 2),),
        (5, 1): (lambda: virtuals(4), lambda: contract(1, 2, 4)),
        (6, 0): (lambda: take_rows(2), lambda: spread_occ(2)),
        (6, 1): (lambda: virtuals(5), lambda: contract(2, 0, 4), lambda: spread_occ(3)),
    }
    for step in range(1, STEPS + 1):
        for chunk in range(2):
            if step == 1:
                take_half(chunk)
            for way in range(2):
                if step > 1:
                    hop(way, step - 1, chunk).wait_recv()
                hop(way, step, chunk).start()
            for work in under.get((step, chunk), ()):
                work()
    take_rows(3)
    for chunk in range(2):
        for way in range(2):
            hop(way, STEPS, chunk).wait_recv()
    virtuals(STEPS)
    contract(3, 0, 4)
    rows = jnp.concatenate([tiles[i, c] for i in range(TIMES) for c in range(2)], axis=1)
    gram = mul(rows, mixed[...].reshape(TIMES * WIDTH, SLOTS))
    term = low(jnp.transpose(gram))
    for m in range(MOST // 2):
        value = mul(term[:, 128 * m : 128 * m + 128], wide[m])
        for b in range(2 * MOST):
            upper, lower = value[32 * b : 32 * b + 16], value[32 * b + 16 : 32 * b + 32]
            for n in range(2):
                lanes = slice(128 * n, 128 * n + 128)
                after = slice(256 + 128 * n, 384 + 128 * n)
                folded[b, 2 * m + n] = low(upper[:, lanes] + lower[:, after])
    for d in range(PAIRS):
        terms[d] = folded[slot_of[d // 2] * 2 + d % 2]

    def trade(axis, count, src, dst, send, recv):
        here = lax.axis_index(axis)

        def one(i):
            peer = lax.rem(here + i, count)
            return pltpu.make_async_remote_copy(
                src_ref=src.at[peer],
                dst_ref=dst.at[here],
                send_sem=send.at[i],
                recv_sem=recv.at[i],
                device_id={axis: peer},
                device_id_type=MESH,
            )

        def begin(i, carry):
            one(i).start()
            return carry

        def end(i, carry):
            one(i).wait()
            return carry

        lax.fori_loop(1, count, begin, 0)
        dst[here] = src[here]
        return lambda: lax.fori_loop(1, count, end, 0)

    arrive = trade("tensor", PAIRS, terms, inbox, send2, recv2)
    inbox[PAIRS, 0] = jnp.zeros((16, 128), jnp.bfloat16)

    def locate(c, carry):
        name = lists_ref[c, block]
        rank = jnp.int32(0)
        for q in range(PB):
            named = lists_ref[0, q] == name
            for other in range(1, CAPS):
                named = named | (lists_ref[other, q] == name)
            places[0, c * PB + q] = jnp.where(named, name, PAIRS)
            places[1, c * PB + q] = jnp.where(named, jnp.minimum(rank, MOST - 1), 0)
            rank = rank + named.astype(jnp.int32)
        return carry

    lax.fori_loop(0, CAPS, locate, 0)
    for step in range(1, STEPS + 1):
        for chunk in range(2):
            for way in range(2):
                hop(way, step, chunk).wait_send()
    arrive()
    for q in range(PB):
        total = inbox[places[0, q], places[1, q]].astype(jnp.float32)
        for c in range(1, CAPS):
            spot = c * PB + q
            total += inbox[places[0, spot], places[1, spot]].astype(jnp.float32)
        chi[q] = low(total)

    trade("tm", TIMES, chi, times, send3, recv3)()
    series = times[...].reshape(TIMES * 16, 128)
    total = mul(waves[:, :WIDTH], series) + mul(waves[:, WIDTH:], series)
    spread[...] = low(total).reshape(TIMES, 16, 128)
    trade("tm", TIMES, spread, freqs, send4, recv4)()

    out_ref[...] = freqs[...]


def unfold_kernel(freqs_ref, out_ref):
    first = iota((16, 128), 1) < 64
    for m in range(PB // 2):
        even = freqs_ref[2 * m].astype(jnp.float32)
        odd = freqs_ref[2 * m + 1].astype(jnp.float32)
        lanes = slice(128 * m, 128 * m + 128)
        out_ref[0, 0:16, lanes] = jnp.where(first, even, pltpu.roll(odd, 64, 1))
        out_ref[0, 16:32, lanes] = jnp.where(first, pltpu.roll(even, 64, 1), odd)


def per_device(integrals, pair_lists, occ_density, virt_density, cosine_weights, coulomb_blocks):
    smem = pl.BlockSpec(memory_space=pltpu.SMEM)
    vmem = pl.BlockSpec(memory_space=pltpu.VMEM)
    hbm = pl.BlockSpec(memory_space=pl.ANY)
    dma = pltpu.SemaphoreType.DMA
    half = jnp.bfloat16
    direct = len(DIRECT)
    block = pltpu.VMEM((PB, 16, 128), half)
    near = pltpu.VMEM((PB + 1, 64, HALF), half)
    arrived = pltpu.VMEM((PB + 1, 64, WIDTH), half)
    freqs = pl.pallas_call(
        kernel,
        out_shape=jax.ShapeDtypeStruct((PB, 16, 128), half),
        in_specs=[smem, vmem, hbm, hbm, vmem, vmem],
        out_specs=vmem,
        scratch_shapes=[
            pltpu.VMEM((direct, ROWS * CAPS, WIDTH), half),
            pltpu.VMEM((PAIRS * ROWS, ROWS * CAPS), half),
            pltpu.VMEM((2, PAIRS, ROWS, HALF), half),
            pltpu.VMEM((direct - 1, PAIRS, ROWS, WIDTH), half),
            near,
            near,
            arrived,
            arrived,
            arrived,
            pltpu.VMEM((TIMES, 2, SLOTS, HALF), half),
            pltpu.VMEM((PB, 64, 64), jnp.float32),
            pltpu.VMEM((1024, 1024), half),
            pltpu.VMEM((HALF, HALF), half),
            pltpu.VMEM((MOST // 2, 128, 512), half),
            pltpu.VMEM((4, 1024, SLOTS), jnp.float32),
            pltpu.VMEM((ORB, ORB, SLOTS), half),
            pltpu.VMEM((ORB, ORB, SLOTS), half),
            pltpu.VMEM((2 * MOST, MOST, 16, 128), half),
            pltpu.VMEM((PAIRS, MOST, 16, 128), half),
            pltpu.VMEM((PAIRS + 1, MOST, 16, 128), half),
            block,
            block,
            block,
            block,
            pltpu.VMEM((WIDTH, 2 * WIDTH), half),
            pltpu.SMEM((2, CAPS * PB), jnp.int32),
            dma((direct,)),
            dma,
            dma((2, PAIRS)),
            dma((2, PAIRS)),
            dma((direct - 1, PAIRS)),
            dma((direct - 1, PAIRS)),
            dma((2, STEPS, 2)),
            dma((2, STEPS, 2)),
            dma((PAIRS,)),
            dma((PAIRS,)),
            dma((TIMES,)),
            dma((TIMES,)),
            dma((TIMES,)),
            dma((TIMES,)),
        ],
        compiler_params=pltpu.CompilerParams(collective_id=0, has_side_effects=True),
        name="polarizability",
    )(
        pair_lists.T, cosine_weights, integrals.reshape(ROWS * CAPS, PB * WIDTH), coulomb_blocks,
        occ_density[0, 0], virt_density[0, 0],
    )
    return pl.pallas_call(
        unfold_kernel,
        out_shape=jax.ShapeDtypeStruct((1, ROWS, PB * 64), jnp.float32),
        in_specs=[vmem],
        out_specs=vmem,
        name="unfold",
    )(freqs)


def solution(mesh):
    in_specs = (
        P("tensor", None, None),
        P(),
        P("tm", "tensor", None, None),
        P("tm", "tensor", None, None),
        P(),
        P(),
    )
    return jax.shard_map(
        per_device, mesh=mesh, in_specs=in_specs, out_specs=P("tm", "tensor", None), check_vma=False
    )
```
